32 devices in a mesh: grp: 4 (over x, core), mem: 8 (over z, y).
Axes of the slice: x: 2, y: 2, z: 4, core: 2. Of those that a mesh axis runs over, the one named last changes fastest.
Arguments:
- perturb: float32 [32, 1024, 1024], P(('grp', 'mem')), may hold values from -0.1875 to 0.1875
- touched_vertex_index: int32 [32, 4, 64], P(('grp', 'mem')), may hold values from 0 to 1023
- proposed_spin_values: int32 [32, 4, 64], P(('grp', 'mem')), may hold values from 0 to 1
- accept: int32 [32, 4, 64], P(('grp', 'mem')), may hold values 0 or 1
- vertex_site_index: int32 [32, 1024], P(('grp', 'mem')), may hold values from 0 to 63
- vertex_time_index: int32 [32, 1024], P(('grp', 'mem')), may hold values from 0 to 4095
- left_proj: float32 [64, 1024], replicated, may hold values from -0.06 to 0.06
- right_proj: float32 [64, 1024], replicated, may hold values from -0.06 to 0.06
- weights: float32 [32], P(('grp', 'mem')), may hold values from 0.3 to 3
- routing: int32 [32, 1], P(('grp', 'mem')), may hold values from 0 to 7; in each aligned block of 8 rows (0 to 7, 8 to 15, ...) at most 2 rows name the same one
- vertex_function_total: float32 [16, 4096, 4096], P('grp', 'mem'), may hold values from -6 to 6
Outputs:
- four_point_out: float32 [16, 4096, 4096], P('grp', 'mem')
The draws below stay inside these ranges and needn't reach their ends.
Inputs may be any that keep to these rules, and one draw needn't show every extreme that they name: `routing`: among the 8 walkers of one group no member index is named by more than 2 walkers, and in some group one index is named by exactly 2.
All inputs are finite; a program needn't handle non-finite values. No bound on the sum of `accept` on one device may be relied on, other than what follows from the above.
Results may differ from the reference program's by a relative error of at most 0.0003.
Values sent between devices are 32-bit elements; how exact they have to be, the bound alone decides.
A program may use at most 128 MiB of HBM per device.

```python
import math
import jax
import jax.numpy as jnp
import numpy as np
from jax import lax

K = 1024
SITES = 64
LEG = 64
Q = 16
TIMES = 4096
RANKB = 64
UPDATES = 4
CAP = 2
ORDER = 4096
WALKERS = 32
N_GRP = 4
N_MEM = 8


def place_ends(array, rng, least, top_value):
    index_at = [jax.random.randint(jax.random.fold_in(rng, axis), (), 0, length) for axis, length in enumerate(array.shape)]
    main_axis = array.shape.index(max(array.shape))
    next_to = index_at[:main_axis] + [(index_at[main_axis] + 1) % array.shape[main_axis]] + index_at[main_axis + 1:]
    return array.at[tuple(index_at)].set(least).at[tuple(next_to)].set(top_value)


def shard_levels(rng, shape, cuts, least, largest):
    def one(axis_at, shards_of):
        steps = jax.random.uniform(jax.random.fold_in(jax.random.fold_in(rng, 6), axis_at), (shards_of,), jnp.float32, least / len(cuts), largest / len(cuts))
        return jnp.repeat(jnp.exp(steps), shape[axis_at] // shards_of).reshape((-1,) + (1,) * (len(shape) - axis_at - 1))

    level = one(*cuts[0])
    for cut in cuts[1:]:
        level = level * one(*cut)
    return level


def assign_block(stream_key, own, number, rows, number_of, top, most, skew):
    sequence = jax.random.permutation(stream_key, number_of)
    crowded, common = portions_of(number_of, rows * top, most, skew, True), portions_of(number_of, rows * top, most, skew, False)
    places = jnp.arange(number_of)

    def named(lengths, rotation):
        used = int((lengths > 0).sum())
        fixed = max(1, used // 4)
        passed = fixed + (places - fixed + rotation * (used - fixed)) % max(1, number_of - fixed)
        return jnp.zeros((number_of,), jnp.int32).at[sequence[jnp.where(places < fixed, places, passed)]].set(jnp.asarray(lengths, jnp.int32))

    lengths = jnp.where(number % 4 == 0, named(crowded, number // 4), named(common, number - number // 4 - 1))
    mixed = jax.random.permutation(jax.random.fold_in(own, 3), number_of)
    giver, sink = mixed[0:number_of // 2 * 2:2], mixed[1:number_of // 2 * 2:2]
    slack = jnp.minimum(lengths[giver] - 1, most - lengths[sink]) // 2
    slack = jnp.where((giver == sequence[0]) | (sink == sequence[0]) | (lengths[sink] == 0), 0, jnp.maximum(slack, 0))
    passed = jax.random.randint(jax.random.fold_in(own, 4), (number_of // 2,), 0, 1 << 20) % (slack + 1)
    lengths = lengths.at[giver].add(-passed).at[sink].add(passed)
    items = jnp.searchsorted(jnp.cumsum(lengths), jnp.arange(rows * top), side="right").astype(jnp.int32)
    listing = items.reshape(top, rows).T
    listing = listing[jax.random.permutation(jax.random.fold_in(own, 1), rows)]
    rotation = jax.random.randint(jax.random.fold_in(own, 2), (rows, 1), 0, top)
    return jnp.take_along_axis(listing, (jnp.arange(top)[None, :] + rotation) % top, axis=1)


def portions_of(amount, total, reach, skew, full):
    loads = [(1 << 20) // math.isqrt(rank ** skew) + 1 for rank in range(1, amount + 1)]
    largest = reach if full else min(reach, max(-(-total // amount), total * loads[0] // sum(loads)))
    least = 1 if total - largest >= amount - 1 else 0
    counts, spare = [largest] + [least] * (amount - 1), total - largest - least * (amount - 1)
    while spare > 0:
        candidates = [i for i in range(1, amount) if counts[i] < largest] or [i for i in range(1, amount) if counts[i] < reach]
        whole, left = sum([loads[i] for i in candidates]), spare
        for i in candidates:
            addition = min(reach - counts[i], max(1, left * loads[i] // whole), spare)
            counts[i] = counts[i] + addition
            spare = spare - addition
    return np.array(counts)


def centred(stream_key, dims, scale, reach, cuts=(), kind=jnp.bfloat16):
    array = scale * jax.random.normal(stream_key, dims, jnp.float32)
    if cuts:
        array = array * shard_levels(stream_key, dims, cuts, -0.22, 0.18)
    return jnp.clip(array, -reach, reach).astype(kind)


def setup_inputs(seed: int = 0) -> dict:
    key_list = jax.random.split(jax.random.key(seed), 12)
    perturb = centred(key_list[0], (WALKERS, K, K), K ** -0.5, 0.1875, ((0, 32),), jnp.float32)
    touched_vertex_index = place_ends(jax.random.randint(key_list[1], (WALKERS, UPDATES, RANKB), 0, K), jax.random.fold_in(key_list[1], 1), 0, K - 1).astype(jnp.int32)
    proposed_spin_values = place_ends(jax.random.randint(key_list[2], (WALKERS, UPDATES, RANKB), 0, 2), jax.random.fold_in(key_list[2], 1), 0, 1).astype(jnp.int32)
    accept = place_ends((jax.random.randint(key_list[3], (WALKERS, UPDATES, RANKB), 0, 4) < 3).astype(jnp.int32), jax.random.fold_in(key_list[3], 1), 0, 1)
    vertex_site_index = place_ends(jax.random.randint(key_list[4], (WALKERS, K), 0, SITES), jax.random.fold_in(key_list[4], 1), 0, SITES - 1).astype(jnp.int32)
    vertex_time_index = place_ends(jax.random.randint(key_list[5], (WALKERS, K), 0, TIMES), jax.random.fold_in(key_list[5], 1), 0, TIMES - 1).astype(jnp.int32)
    left_proj = centred(key_list[6], (SITES, LEG * Q), 0.01, 0.06, (), jnp.float32)
    right_proj = centred(key_list[7], (SITES, LEG * Q), 0.01, 0.06, (), jnp.float32)
    weights = jnp.clip(jnp.exp(math.log(3.0) - 2.3025851 * jax.random.uniform(key_list[8], (WALKERS,), jnp.float32) ** shard_levels(key_list[8], (WALKERS,), ((0, 32),), -0.2, 0.2)), 0.3, 3.0)
    routing_keys = jax.random.split(jax.random.fold_in(key_list[9], 1), WALKERS // N_MEM)
    routing_turns = jax.random.permutation(jax.random.fold_in(key_list[9], 3), WALKERS // N_MEM)
    routing = jax.vmap(lambda own, number: assign_block(jax.random.fold_in(key_list[9], 2), own, number, N_MEM, N_MEM, 1, CAP, 2))(routing_keys, routing_turns).reshape((WALKERS, 1))
    vertex_function_total = centred(key_list[10], (Q, ORDER, ORDER), 1.0, 6.0, ((0, 4), (1, 8)), jnp.float32)
    return {"perturb": perturb, "touched_vertex_index": touched_vertex_index, "proposed_spin_values": proposed_spin_values, "accept": accept, "vertex_site_index": vertex_site_index, "vertex_time_index": vertex_time_index, "left_proj": left_proj, "right_proj": right_proj, "weights": weights, "routing": routing, "vertex_function_total": vertex_function_total}


EXACT_ARITHMETIC = lax.Precision.HIGHEST

def legendre(time_ids):
    abscissa = (2.0 * time_ids.astype(jnp.float32) + 1.0) / TIMES - 1.0
    polys = [jnp.ones_like(abscissa), abscissa]
    for degree in range(1, LEG - 1):
        polys.append(((2 * degree + 1) * abscissa * polys[degree] - degree * polys[degree - 1]) / (degree + 1))
    norms = jnp.sqrt(2.0 * jnp.arange(LEG, dtype=jnp.float32) + 1.0)
    return jnp.stack(polys[:LEG], axis=1) * norms[None, :]

def make_onehot(site_ids):
    return (site_ids[:, None] == jnp.arange(SITES, dtype=jnp.int32)[None, :]).astype(jnp.float32)

def project(onehot, polys, table):
    spread = jnp.dot(onehot, table, precision=EXACT_ARITHMETIC, preferred_element_type=jnp.float32)
    return lax.optimization_barrier(jnp.sum(spread.reshape(-1, LEG, Q) * polys[:, :, None], axis=1))

def transform(onehot, polys, values):
    weighted = (polys[:, :, None] * values[:, None, :]).reshape(-1, LEG * Q)
    summed = jnp.dot(onehot.T, weighted, precision=EXACT_ARITHMETIC, preferred_element_type=jnp.float32)
    return summed.reshape(SITES, LEG, Q).transpose(2, 0, 1).reshape(Q, SITES * LEG)

def update_walker(perturb, touched_vertex_index, proposed_spin_values, accept):
    matrix = jnp.eye(K, dtype=jnp.float32) + perturb
    gammas = accept.astype(jnp.float32) * jnp.where(proposed_spin_values == 1, 0.6, -0.4).astype(jnp.float32)
    positions = jnp.arange(K, dtype=jnp.int32)

    def apply_update(update, matrix):
        chosen = touched_vertex_index[update]
        unit_cols = (positions[:, None] == chosen[None, :]).astype(jnp.float32)
        columns = (jnp.take(matrix, chosen, axis=1) - unit_cols) * gammas[update][None, :]
        row_block = jnp.take(matrix, chosen, axis=0)
        return matrix - jnp.dot(columns, row_block, precision=EXACT_ARITHMETIC, preferred_element_type=jnp.float32)
    return lax.fori_loop(0, UPDATES, apply_update, matrix)

def measure_one(perturb, touched_vertex_index, proposed_spin_values, accept, vertex_site_index, vertex_time_index, left_proj, right_proj):
    matrix = update_walker(perturb, touched_vertex_index, proposed_spin_values, accept)
    polys = legendre(vertex_time_index)
    onehot = make_onehot(vertex_site_index)
    left_vec = project(onehot, polys, left_proj)
    right_vec = project(onehot, polys, right_proj)
    left_image = jnp.dot(matrix, left_vec, precision=EXACT_ARITHMETIC, preferred_element_type=jnp.float32)
    right_image = jnp.dot(matrix.T, right_vec, precision=EXACT_ARITHMETIC, preferred_element_type=jnp.float32)
    return (transform(onehot, polys, left_image), transform(onehot, polys, right_image))

def reference(perturb, touched_vertex_index, proposed_spin_values, accept, vertex_site_index, vertex_time_index, left_proj, right_proj, weights, routing, vertex_function_total):

    def single_walker_result(inputs):
        return measure_one(inputs[0], inputs[1], inputs[2], inputs[3], inputs[4], inputs[5], left_proj, right_proj)
    left_observed, right_observed = lax.map(single_walker_result, (perturb, touched_vertex_index, proposed_spin_values, accept, vertex_site_index, vertex_time_index))
    targets = routing[:, 0]
    member_mask = (targets[:, None] == jnp.arange(N_MEM, dtype=jnp.int32)[None, :]).astype(jnp.float32)
    members = member_mask * weights[:, None]
    totals = members.reshape(N_GRP, N_MEM, N_MEM).sum(axis=1)
    group_totals = jnp.repeat(totals, N_MEM, axis=0)
    own_total = lax.optimization_barrier(jnp.sum(group_totals * member_mask, axis=1))
    gamma_factor_list = weights / own_total
    rescaled_rows = left_observed * gamma_factor_list[:, None, None]
    return vertex_function_total + jnp.einsum('npa,npk->pak', rescaled_rows, right_observed, precision=EXACT_ARITHMETIC)
```

```python
import functools
import math

import jax
import jax.numpy as jnp
from jax import lax
from jax.experimental import pallas as pl
from jax.experimental.pallas import tpu as pltpu
from jax.sharding import PartitionSpec as P

TIMES = 4096
LANES = 128
F32 = jnp.float32
BF16 = jnp.bfloat16
NN = (((1,), (0,)), ((), ()))
NT = (((1,), (1,)), ((), ()))
TN = (((0,), (0,)), ((), ()))


def split(x):
    hi = x.astype(BF16)
    return hi, (x - hi.astype(F32)).astype(BF16)


def dot(a, b, dims=NN):
    return lax.dot_general(a, b, dims, preferred_element_type=F32)


def dot_exact(a, b, dims=NN):
    return lax.dot_general(a, b, dims, precision=lax.Precision.HIGHEST, preferred_element_type=F32)


def legendre_rows(times, legs):
    x = (2.0 * times + 1.0) * (1.0 / TIMES) - 1.0
    before, now = jnp.ones_like(x), x
    yield before
    yield now * math.sqrt(3.0)
    for d in range(1, legs - 1):
        before, now = now, ((2 * d + 1) / (d + 1)) * (x * now) - (d / (d + 1)) * before
        yield now * math.sqrt(2.0 * (d + 1) + 1.0)


def measure_kernel(
    n_grp, legs, updates,
    perturb, columns, site, time, left_proj, right_proj, weight, routing,
    out, polys, spread,
):
    order = perturb.shape[1]
    sites, width = left_proj.shape
    q = width // legs
    per = q // n_grp
    touched = columns.shape[0]
    rank = touched // updates
    for d, row in enumerate(legendre_rows(time[...].astype(F32), legs)):
        polys[d : d + 1, :] = row
    onehot = (lax.broadcasted_iota(jnp.int32, (sites, order), 0) == site[...]).astype(BF16)
    onehot2 = jnp.concatenate([onehot, onehot], axis=0)
    vectors = []
    for table in (left_proj, right_proj):
        hi, lo = split(table[...])
        spread[...] = dot(jnp.concatenate([hi, lo], axis=0), onehot2, TN)
        total = jnp.zeros((q, order), F32)
        for d in range(legs):
            total = total + spread[d * q : (d + 1) * q, :] * polys[d : d + 1, :]
        vectors.append(total)
    left_vec, right_vec = vectors

    index = columns[:, 0:1]
    gammas = columns[:, 2:3].astype(F32) * jnp.where(columns[:, 1:2] == 1, 0.6, -0.4)
    select = (lax.broadcasted_iota(jnp.int32, (touched, order), 1) == index).astype(BF16)
    p_hi, p_lo = split(perturb[0])
    l_hi, l_lo = split(left_vec)
    r_hi, r_lo = split(right_vec)
    rows = jnp.concatenate([select, r_hi, r_lo], axis=0)
    cols = jnp.concatenate([select, l_hi, l_lo], axis=0)
    by_rows = dot(rows, p_hi) + dot(rows, p_lo)
    by_cols = dot(cols, p_hi, NT) + dot(cols, p_lo, NT)
    p_rows, p_cols = by_rows[:touched], by_cols[:touched]
    g = by_rows[touched : touched + q] + by_rows[touched + q :]
    w = left_vec + by_cols[touched : touched + q] + by_cols[touched + q :]

    def picked(x):
        hi, lo = split(x)
        return dot(hi, select, NT) + dot(lo, select, NT)

    kernel = picked(p_rows)
    overlap = kernel + dot(select, select, NT)
    eye = (
        lax.broadcasted_iota(jnp.int32, (touched, touched), 0)
        == lax.broadcasted_iota(jnp.int32, (touched, touched), 1)
    ).astype(F32)
    s = jnp.zeros((touched, touched), F32)
    for u in range(updates):
        part = slice(u * rank, (u + 1) * rank)
        if u == 0:
            first, second = eye[:, part], eye[part, :]
        else:
            first = eye[:, part] - dot_exact(s, overlap[:, part])
            second = eye[part, :] - dot_exact(kernel[part, :], s)
        s = s + dot_exact(first, gammas[part, :] * second)
    z = dot_exact(picked(w), s, NT)
    v = dot_exact(picked(g), s)
    left_image = w - dot_exact(z, p_cols)
    v_hi, v_lo = split(v)
    right_image = right_vec + g - (dot_exact(v, p_rows) + dot(v_hi, select) + dot(v_lo, select))

    tiles = order // LANES
    site_f, time_f = site[...].astype(F32), time[...].astype(F32)
    for t in range(tiles):
        lanes = slice(t * LANES, (t + 1) * LANES)
        for k in range(n_grp):
            mine = slice(k * per, (k + 1) * per)
            out[k, t * 2 * per : t * 2 * per + per, :] = left_image[mine, lanes]
            out[k, t * 2 * per + per : (t + 1) * 2 * per, :] = right_image[mine, lanes]
            base = tiles * 2 * per
            out[k, base + t : base + t + 1, :] = site_f[:, lanes]
            out[k, base + tiles + t : base + tiles + t + 1, :] = time_f[:, lanes]
    base = tiles * (2 * per + 2)
    for k in range(n_grp):
        out[k, base : base + 4, :] = jnp.full((4, LANES), weight[0], F32)
        out[k, base + 4 : base + 8, :] = jnp.full((4, LANES), routing[0, 0].astype(F32), F32)


def accumulate_kernel(
    legs, per, tiles, blocks,
    gathered, total_in, out, polys, left_rows, right_rows, table, images, right_pair,
):
    n_mem, n_grp = gathered.shape[0], gathered.shape[1]
    walkers = n_mem * n_grp
    pairs = total_in.shape[2] // LANES
    step = pl.program_id(0)
    mem = lax.axis_index("mem")
    meta = tiles * 2 * per
    last = meta + 2 * tiles

    @pl.when(step == 0)
    def _():
        def member(m, carry):
            times = jnp.concatenate(
                [gathered[m, g, meta + tiles : last, :] for g in range(n_grp)], axis=0
            )
            for d, row in enumerate(legendre_rows(times, legs)):
                polys[d * n_grp * tiles : (d + 1) * n_grp * tiles, :] = row
            for g in range(n_grp):
                walker = m * n_grp + g
                own = gathered[m, g, last + 4 : last + 5, :]
                weight = gathered[m, g, last : last + 1, :]
                same = jnp.zeros_like(own)
                for other in range(n_mem):
                    same = same + jnp.where(
                        gathered[other, g, last + 4 : last + 5, :] == own,
                        gathered[other, g, last : last + 1, :],
                        0.0,
                    )
                factor = weight / same
                for t in range(tiles):
                    lanes = slice(t * LANES, (t + 1) * LANES)
                    site = gathered[m, g, meta + t : meta + t + 1, :].astype(jnp.int32)
                    odd, pair = site % 2, site // 2
                    p = polys[pl.ds(g * tiles + t, legs, stride=n_grp * tiles), :]
                    p = jnp.concatenate(
                        [jnp.where(odd == 0, p, 0.0), jnp.where(odd == 1, p, 0.0)], axis=0
                    )
                    p_hi, p_lo = split(p)
                    table[:LANES, lanes] = p_hi
                    table[LANES:, lanes] = p_lo
                    image = gathered[m, g, t * 2 * per : (t + 1) * 2 * per, :]
                    hi = image.astype(BF16).astype(F32)
                    lo = image - hi
                    at = pair == lax.broadcasted_iota(jnp.int32, (pairs, LANES), 0)
                    at_own = pair == mem * blocks + lax.broadcasted_iota(jnp.int32, (8, LANES), 0)
                    half = per * pairs + per * 8
                    for part, value in ((0, hi), (1, lo)):
                        rows = [jnp.where(at, value[per + k : per + k + 1, :], 0.0) for k in range(per)]
                        rows += [jnp.where(at_own, value[k : k + 1, :], 0.0) for k in range(per)]
                        images[part * half : (part + 1) * half, lanes] = jnp.concatenate(
                            rows, axis=0
                        ).astype(BF16)
                half = per * pairs + per * 8
                both = dot(images[...], table[...], NT)
                summed = both[:half, :LANES] + both[:half, LANES:] + both[half:, :LANES]
                for k in range(per):
                    right_rows[pl.ds(k * pairs * walkers + walker, pairs, stride=walkers), :] = (
                        summed[k * pairs : (k + 1) * pairs, :]
                    )
                    for b in range(blocks):
                        at_row = per * pairs + k * 8 + b
                        left_rows[pl.ds((k * blocks + b) * walkers + walker, 1), :] = (
                            summed[at_row : at_row + 1, :] * factor
                        )
            return carry

        lax.fori_loop(0, n_mem, member, 0)

    transfer, block = step // blocks, step % blocks

    @pl.when(block == 0)
    def _():
        for c in range(pairs):
            start = pl.multiple_of((transfer * pairs + c) * walkers, walkers)
            hi, lo = split(right_rows[pl.ds(start, walkers), :])
            lanes = slice(c * LANES, (c + 1) * LANES)
            right_pair[:walkers, lanes] = hi
            right_pair[walkers : 2 * walkers, lanes] = lo
            right_pair[2 * walkers :, lanes] = hi

    start = pl.multiple_of((transfer * blocks + block) * walkers, walkers)
    hi, lo = split(left_rows[pl.ds(start, walkers), :])
    left = jnp.concatenate([hi, hi, lo], axis=0)
    out[0] = total_in[0] + dot(left, right_pair[...], TN)


def gather_payload(payload):
    swapped = lax.all_to_all(payload, "grp", split_axis=0, concat_axis=0, tiled=True)
    return lax.all_gather(swapped, "mem", axis=0)


def per_device(
    n_grp, n_mem,
    perturb, touched_vertex_index, proposed_spin_values, accept,
    vertex_site_index, vertex_time_index, left_proj, right_proj,
    weights, routing, vertex_function_total,
):
    order = perturb.shape[1]
    sites, width = left_proj.shape
    per, rows, cols = vertex_function_total.shape
    legs = cols // sites
    updates, rank = touched_vertex_index.shape[1:]
    tiles = order // LANES
    blocks = rows // LANES
    payload_rows = tiles * (2 * per + 2) + 8
    columns = jnp.stack(
        [touched_vertex_index[0], proposed_spin_values[0], accept[0]], axis=-1
    ).reshape(updates * rank, 3)
    vmem = pl.BlockSpec(memory_space=pltpu.VMEM)
    smem = pl.BlockSpec(memory_space=pltpu.SMEM)
    payload = pl.pallas_call(
        functools.partial(measure_kernel, n_grp, legs, updates),
        out_shape=jax.ShapeDtypeStruct((n_grp, payload_rows, LANES), F32),
        in_specs=[vmem] * 6 + [smem] * 2,
        out_specs=vmem,
        scratch_shapes=[pltpu.VMEM((legs, order), F32), pltpu.VMEM((width, order), F32)],
        compiler_params=pltpu.CompilerParams(vmem_limit_bytes=48 * 2**20),
    )(perturb, columns, vertex_site_index, vertex_time_index, left_proj, right_proj, weights, routing)
    gathered = gather_payload(payload)
    walkers = n_grp * n_mem
    pairs = cols // LANES
    return pl.pallas_call(
        functools.partial(accumulate_kernel, legs, per, tiles, blocks),
        grid=(per * blocks,),
        out_shape=jax.ShapeDtypeStruct(vertex_function_total.shape, F32),
        in_specs=[
            vmem,
            pl.BlockSpec((1, LANES, cols), lambda i: (i // blocks, i % blocks, 0)),
        ],
        out_specs=pl.BlockSpec((1, LANES, cols), lambda i: (i // blocks, i % blocks, 0)),
        scratch_shapes=[
            pltpu.VMEM((legs * n_grp * tiles, LANES), F32),
            pltpu.VMEM((per * blocks * walkers, LANES), F32),
            pltpu.VMEM((per * pairs * walkers, LANES), F32),
            pltpu.VMEM((2 * LANES, order), BF16),
            pltpu.VMEM((2 * (per * pairs + per * 8), order), BF16),
            pltpu.VMEM((3 * walkers, cols), BF16),
        ],
        compiler_params=pltpu.CompilerParams(vmem_limit_bytes=56 * 2**20),
    )(gathered, vertex_function_total)


def solution(mesh):
    in_specs = (
        P(("grp", "mem"), None, None),
        P(("grp", "mem"), None, None),
        P(("grp", "mem"), None, None),
        P(("grp", "mem"), None, None),
        P(("grp", "mem"), None),
        P(("grp", "mem"), None),
        P(),
        P(),
        P(("grp", "mem")),
        P(("grp", "mem"), None),
        P("grp", "mem", None),
    )
    return jax.shard_map(
        functools.partial(per_device, mesh.shape["grp"], mesh.shape["mem"]),
        mesh=mesh, in_specs=in_specs, out_specs=P("grp", "mem", None), check_vma=False,
    )
```

```python
import functools
import math

import jax
import jax.numpy as jnp
from jax import lax
from jax.experimental import pallas as pl
from jax.experimental.pallas import tpu as pltpu
from jax.sharding import PartitionSpec as P

TIMES = 4096
LANES = 128
F32 = jnp.float32
BF16 = jnp.bfloat16
NN = (((1,), (0,)), ((), ()))
NT = (((1,), (1,)), ((), ()))
MESH = pl.DeviceIdType.MESH
TN = (((0,), (0,)), ((), ()))


def split(x):
    hi = x.astype(BF16)
    return hi, (x - hi.astype(F32)).astype(BF16)


def dot(a, b, dims=NN):
    return lax.dot_general(a, b, dims, preferred_element_type=F32)


def dot_exact(a, b, dims=NN):
    return lax.dot_general(a, b, dims, precision=lax.Precision.HIGHEST, preferred_element_type=F32)


def legendre_rows(times, legs):
    x = (2.0 * times + 1.0) * (1.0 / TIMES) - 1.0
    before, now = jnp.ones_like(x), x
    yield before
    yield now * math.sqrt(3.0)
    for d in range(1, legs - 1):
        before, now = now, ((2 * d + 1) / (d + 1)) * (x * now) - (d / (d + 1)) * before
        yield now * math.sqrt(2.0 * (d + 1) + 1.0)


def measure_kernel(
    n_grp, legs, updates,
    perturb_in, touched_in, spins_in, accept_in, site_in, time_in, left_in, right_in, weight, routing,
    out, polys, spread, perturb, chosen, spins, accept, site, time, left_proj, right_proj, arrived,
):
    loads = []
    for k, (source, target) in enumerate((
        (time_in, time), (site_in, site), (left_in, left_proj), (right_in, right_proj),
        (touched_in, chosen), (spins_in, spins), (accept_in, accept), (perturb_in, perturb),
    )):
        loads.append(pltpu.make_async_copy(source, target, arrived.at[k]))
        loads[-1].start()
    order = perturb.shape[1]
    sites, width = left_proj.shape
    q = width // legs
    per = q // n_grp
    rank = chosen.shape[2]
    touched = updates * rank
    for load in loads[:4]:
        load.wait()
    for d, row in enumerate(legendre_rows(time[...].astype(F32), legs)):
        polys[d : d + 1, :] = row
    onehot = (lax.broadcasted_iota(jnp.int32, (sites, order), 0) == site[...]).astype(BF16)
    onehot2 = jnp.concatenate([onehot, onehot], axis=0)
    vectors = []
    for table in (left_proj, right_proj):
        hi, lo = split(table[...])
        spread[...] = dot(jnp.concatenate([hi, lo], axis=0), onehot2, TN)
        total = jnp.zeros((q, order), F32)
        for d in range(legs):
            total = total + spread[d * q : (d + 1) * q, :] * polys[d : d + 1, :]
        vectors.append(total)
    left_vec, right_vec = vectors

    for load in loads[4:]:
        load.wait()
    square = lax.broadcasted_iota(jnp.int32, (rank, rank), 0) == lax.broadcasted_iota(
        jnp.int32, (rank, rank), 1
    )

    def column(rows):
        parts = [
            jnp.sum(jnp.where(square, rows[u : u + 1, :].astype(F32), 0.0), axis=1, keepdims=True)
            for u in range(updates)
        ]
        return jnp.concatenate(parts, axis=0)

    index = column(chosen[0]).astype(jnp.int32)
    gammas = column(accept[0].astype(F32) * jnp.where(spins[0] == 1, 0.6, -0.4))
    select = (lax.broadcasted_iota(jnp.int32, (touched, order), 1) == index).astype(BF16)
    p_hi, p_lo = split(perturb[0])
    l_hi, l_lo = split(left_vec)
    r_hi, r_lo = split(right_vec)
    rows = jnp.concatenate([select, r_hi, r_lo], axis=0)
    cols = jnp.concatenate([select, l_hi, l_lo], axis=0)
    by_rows = dot(rows, p_hi) + dot(rows, p_lo)
    by_cols = dot(cols, p_hi, NT) + dot(cols, p_lo, NT)
    p_rows, p_cols = by_rows[:touched], by_cols[:touched]
    g = by_rows[touched : touched + q] + by_rows[touched + q :]
    w = left_vec + by_cols[touched : touched + q] + by_cols[touched + q :]

    def picked(x):
        hi, lo = split(x)
        return dot(hi, select, NT) + dot(lo, select, NT)

    kernel = picked(p_rows)
    overlap = kernel + dot(select, select, NT)
    eye = (
        lax.broadcasted_iota(jnp.int32, (touched, touched), 0)
        == lax.broadcasted_iota(jnp.int32, (touched, touched), 1)
    ).astype(F32)
    s = jnp.zeros((touched, touched), F32)
    for u in range(updates):
        part = slice(u * rank, (u + 1) * rank)
        if u == 0:
            first, second = eye[:, part], eye[part, :]
        else:
            first = eye[:, part] - dot_exact(s, overlap[:, part])
            second = eye[part, :] - dot_exact(kernel[part, :], s)
        s = s + dot_exact(first, gammas[part, :] * second)
    z = dot_exact(picked(w), s, NT)
    v = dot_exact(picked(g), s)
    left_image = w - dot_exact(z, p_cols)
    v_hi, v_lo = split(v)
    right_image = right_vec + g - (dot_exact(v, p_rows) + dot(v_hi, select) + dot(v_lo, select))

    tiles = order // LANES
    site_f, time_f = site[...].astype(F32), time[...].astype(F32)
    for t in range(tiles):
        lanes = slice(t * LANES, (t + 1) * LANES)
        for k in range(n_grp):
            mine = slice(k * per, (k + 1) * per)
            out[k, t * 2 * per : t * 2 * per + per, :] = left_image[mine, lanes]
            out[k, t * 2 * per + per : (t + 1) * 2 * per, :] = right_image[mine, lanes]
            base = tiles * 2 * per
            out[k, base + t : base + t + 1, :] = site_f[:, lanes]
            out[k, base + tiles + t : base + tiles + t + 1, :] = time_f[:, lanes]
    base = tiles * (2 * per + 2)
    for k in range(n_grp):
        out[k, base : base + 4, :] = jnp.full((4, LANES), weight[0], F32)
        out[k, base + 4 : base + 8, :] = jnp.full((4, LANES), routing[0, 0].astype(F32), F32)


def accumulate_kernel(
    legs, per, tiles, blocks,
    gathered, total_hbm, out, polys, left_rows, right_rows, table, images, right_pair, held, arrived,
):
    n_mem, n_grp = gathered.shape[0], gathered.shape[1]
    walkers = n_mem * n_grp
    pairs = total_hbm.shape[2] // LANES
    step = pl.program_id(0)
    mem = lax.axis_index("mem")
    meta = tiles * 2 * per
    last = meta + 2 * tiles

    def load(at):
        k, b = at // blocks, at % blocks
        rows = pl.ds(pl.multiple_of(b * LANES, LANES), LANES)
        return pltpu.make_async_copy(total_hbm.at[k, rows, :], held.at[at], arrived.at[at])

    @pl.when(step == 0)
    def _():
        lax.fori_loop(0, per * blocks, lambda at, carry: (load(at).start(), carry)[1], 0)

        def member(m, carry):
            times = jnp.concatenate(
                [gathered[m, g, meta + tiles : last, :] for g in range(n_grp)], axis=0
            )
            for d, row in enumerate(legendre_rows(times, legs)):
                polys[d * n_grp * tiles : (d + 1) * n_grp * tiles, :] = row
            for g in range(n_grp):
                walker = m * n_grp + g
                own = gathered[m, g, last + 4 : last + 5, :]
                weight = gathered[m, g, last : last + 1, :]
                same = jnp.zeros_like(own)
                for other in range(n_mem):
                    same = same + jnp.where(
                        gathered[other, g, last + 4 : last + 5, :] == own,
                        gathered[other, g, last : last + 1, :],
                        0.0,
                    )
                factor = weight / same
                for t in range(tiles):
                    lanes = slice(t * LANES, (t + 1) * LANES)
                    site = gathered[m, g, meta + t : meta + t + 1, :].astype(jnp.int32)
                    odd, pair = site % 2, site // 2
                    p = polys[pl.ds(g * tiles + t, legs, stride=n_grp * tiles), :]
                    p = jnp.concatenate(
                        [jnp.where(odd == 0, p, 0.0), jnp.where(odd == 1, p, 0.0)], axis=0
                    )
                    p_hi, p_lo = split(p)
                    table[:LANES, lanes] = p_hi
                    table[LANES:, lanes] = p_lo
                    image = gathered[m, g, t * 2 * per : (t + 1) * 2 * per, :]
                    hi = image.astype(BF16).astype(F32)
                    lo = image - hi
                    at = pair == lax.broadcasted_iota(jnp.int32, (pairs, LANES), 0)
                    at_own = pair == mem * blocks + lax.broadcasted_iota(jnp.int32, (8, LANES), 0)
                    half = per * pairs + per * 8
                    for part, value in ((0, hi), (1, lo)):
                        rows = [jnp.where(at, value[per + k : per + k + 1, :], 0.0) for k in range(per)]
                        rows += [jnp.where(at_own, value[k : k + 1, :], 0.0) for k in range(per)]
                        images[part * half : (part + 1) * half, lanes] = jnp.concatenate(
                            rows, axis=0
                        ).astype(BF16)
                half = per * pairs + per * 8
                both = dot(images[...], table[...], NT)
                summed = both[:half, :LANES] + both[:half, LANES:] + both[half:, :LANES]
                for k in range(per):
                    right_rows[pl.ds(k * pairs * walkers + walker, pairs, stride=walkers), :] = (
                        summed[k * pairs : (k + 1) * pairs, :]
                    )
                    for b in range(blocks):
                        at_row = per * pairs + k * 8 + b
                        left_rows[pl.ds((k * blocks + b) * walkers + walker, 1), :] = (
                            summed[at_row : at_row + 1, :] * factor
                        )
            return carry

        lax.fori_loop(0, n_mem, member, 0)

    transfer, block = step // blocks, step % blocks

    @pl.when(block == 0)
    def _():
        for c in range(pairs):
            start = pl.multiple_of((transfer * pairs + c) * walkers, walkers)
            hi, lo = split(right_rows[pl.ds(start, walkers), :])
            lanes = slice(c * LANES, (c + 1) * LANES)
            right_pair[:walkers, lanes] = hi
            right_pair[walkers : 2 * walkers, lanes] = lo
            right_pair[2 * walkers :, lanes] = hi

    start = pl.multiple_of((transfer * blocks + block) * walkers, walkers)
    hi, lo = split(left_rows[pl.ds(start, walkers), :])
    left = jnp.concatenate([hi, hi, lo], axis=0)
    load(step).wait()
    out[0] = held[step] + dot(left, right_pair[...], TN)


def gather_kernel(n_grp, n_mem, payload, out, grp_send, grp_recv, ring_send, ring_recv, own_sem):
    grp, mem = lax.axis_index("grp"), lax.axis_index("mem")
    half = n_mem // 2

    def at_place(place):
        return jnp.where(place < half, 2 * place, 2 * (n_mem - 1 - place) + 1)

    place = jnp.where(mem % 2 == 0, mem // 2, n_mem - 1 - mem // 2)
    peers = [
        ((grp // 2 + j // 2) % (n_grp // 2)) * 2 + (grp % 2 + j % 2) % 2 for j in range(n_grp)
    ]
    sides = [at_place((place + 1) % n_mem), at_place((place + n_mem - 1) % n_mem)]

    barrier = pltpu.get_barrier_semaphore()
    for peer in peers[1:]:
        pl.semaphore_signal(barrier, inc=1, device_id=(peer, mem), device_id_type=MESH)
    for side in sides:
        pl.semaphore_signal(barrier, inc=1, device_id=(grp, side), device_id_type=MESH)
    pl.semaphore_wait(barrier, n_grp + 1)

    def runs(step, j):
        if step < half - 1:
            return (0, 1)
        if step == half - 1:
            return (j % 2,)
        return ()

    started = []

    def pass_on(step, j, side, source):
        origin = at_place((place + (n_mem - step if side == 0 else step)) % n_mem)
        copy = pltpu.make_async_remote_copy(
            src_ref=payload.at[peers[j]] if source is None else source,
            dst_ref=out.at[origin, peers[j]],
            send_sem=ring_send.at[side, step, j],
            recv_sem=ring_recv.at[side, step, j],
            device_id=(grp, sides[side]),
            device_id_type=MESH,
        )
        copy.start()
        started.append(copy)

    crossing = []
    for j in range(1, n_grp):
        copy = pltpu.make_async_remote_copy(
            src_ref=payload.at[peers[j]],
            dst_ref=out.at[mem, grp],
            send_sem=grp_send.at[peers[j]],
            recv_sem=grp_recv.at[grp],
            device_id=(peers[j], mem),
            device_id_type=MESH,
        )
        copy.start()
        crossing.append(copy)
    for side in runs(0, 0):
        pass_on(0, 0, side, None)
    own = pltpu.make_async_copy(payload.at[grp], out.at[mem, grp], own_sem)
    own.start()
    for j in range(1, n_grp):
        block = out.at[mem, peers[j]]
        pltpu.make_async_copy(block, block, grp_recv.at[peers[j]]).wait()
        for side in runs(0, j):
            pass_on(0, j, side, block)
    for step in range(1, half + 1):
        for j in range(n_grp):
            for side in runs(step - 1, j):
                origin = at_place((place + (n_mem - step if side == 0 else step)) % n_mem)
                block = out.at[origin, peers[j]]
                pltpu.make_async_copy(block, block, ring_recv.at[side, step - 1, j]).wait()
                if side in runs(step, j):
                    pass_on(step, j, side, block)
    own.wait()
    for copy in crossing + started:
        copy.wait_send()


def gather_payload(payload, n_grp, n_mem):
    half = n_mem // 2
    vmem = pl.BlockSpec(memory_space=pltpu.VMEM)
    return pl.pallas_call(
        functools.partial(gather_kernel, n_grp, n_mem),
        out_shape=jax.ShapeDtypeStruct((n_mem, *payload.shape), F32),
        in_specs=[vmem],
        out_specs=vmem,
        scratch_shapes=[
            pltpu.SemaphoreType.DMA((n_grp,)),
            pltpu.SemaphoreType.DMA((n_grp,)),
            pltpu.SemaphoreType.DMA((2, half, n_grp)),
            pltpu.SemaphoreType.DMA((2, half, n_grp)),
            pltpu.SemaphoreType.DMA,
        ],
        compiler_params=pltpu.CompilerParams(
            collective_id=0, has_side_effects=True, vmem_limit_bytes=(20 if n_mem > 8 else 8) * 2**20
        ),
    )(payload)


def per_device(
    n_grp, n_mem,
    perturb, touched_vertex_index, proposed_spin_values, accept,
    vertex_site_index, vertex_time_index, left_proj, right_proj,
    weights, routing, vertex_function_total,
):
    order = perturb.shape[1]
    sites, width = left_proj.shape
    per, rows, cols = vertex_function_total.shape
    legs = cols // sites
    updates, rank = touched_vertex_index.shape[1:]
    tiles = order // LANES
    blocks = rows // LANES
    payload_rows = tiles * (2 * per + 2) + 8
    vmem = pl.BlockSpec(memory_space=pltpu.VMEM)
    smem = pl.BlockSpec(memory_space=pltpu.SMEM)
    hbm = pl.BlockSpec(memory_space=pl.ANY)
    loaded = (
        perturb, touched_vertex_index, proposed_spin_values, accept,
        vertex_site_index, vertex_time_index, left_proj, right_proj,
    )
    payload = pl.pallas_call(
        functools.partial(measure_kernel, n_grp, legs, updates),
        out_shape=jax.ShapeDtypeStruct((n_grp, payload_rows, LANES), F32),
        in_specs=[hbm] * 8 + [smem] * 2,
        out_specs=vmem,
        scratch_shapes=[pltpu.VMEM((legs, order), F32), pltpu.VMEM((width, order), F32)]
        + [pltpu.VMEM(x.shape, x.dtype) for x in loaded]
        + [pltpu.SemaphoreType.DMA((len(loaded),))],
        compiler_params=pltpu.CompilerParams(vmem_limit_bytes=48 * 2**20),
    )(*loaded, weights, routing)
    gathered = gather_payload(payload, n_grp, n_mem)
    walkers = n_grp * n_mem
    pairs = cols // LANES
    return pl.pallas_call(
        functools.partial(accumulate_kernel, legs, per, tiles, blocks),
        grid=(per * blocks,),
        out_shape=jax.ShapeDtypeStruct(vertex_function_total.shape, F32),
        in_specs=[vmem, hbm],
        out_specs=pl.BlockSpec((1, LANES, cols), lambda i: (i // blocks, i % blocks, 0)),
        scratch_shapes=[
            pltpu.VMEM((legs * n_grp * tiles, LANES), F32),
            pltpu.VMEM((per * blocks * walkers, LANES), F32),
            pltpu.VMEM((per * pairs * walkers, LANES), F32),
            pltpu.VMEM((2 * LANES, order), BF16),
            pltpu.VMEM((2 * (per * pairs + per * 8), order), BF16),
            pltpu.VMEM((3 * walkers, cols), BF16),
            pltpu.VMEM((per * blocks, LANES, cols), F32),
            pltpu.SemaphoreType.DMA((per * blocks,)),
        ],
        compiler_params=pltpu.CompilerParams(vmem_limit_bytes=56 * 2**20),
    )(gathered, vertex_function_total)


def solution(mesh):
    in_specs = (
        P(("grp", "mem"), None, None),
        P(("grp", "mem"), None, None),
        P(("grp", "mem"), None, None),
        P(("grp", "mem"), None, None),
        P(("grp", "mem"), None),
        P(("grp", "mem"), None),
        P(),
        P(),
        P(("grp", "mem")),
        P(("grp", "mem"), None),
        P("grp", "mem", None),
    )
    return jax.shard_map(
        functools.partial(per_device, mesh.shape["grp"], mesh.shape["mem"]),
        mesh=mesh, in_specs=in_specs, out_specs=P("grp", "mem", None), check_vma=False,
    )
```

```python
import functools
import math

import jax
import jax.numpy as jnp
from jax import lax
from jax.experimental import pallas as pl
from jax.experimental.pallas import tpu as pltpu
from jax.sharding import PartitionSpec as P

TIMES = 4096
LANES = 128
F32 = jnp.float32
BF16 = jnp.bfloat16
NN = (((1,), (0,)), ((), ()))
NT = (((1,), (1,)), ((), ()))
MESH = pl.DeviceIdType.MESH
TN = (((0,), (0,)), ((), ()))


def split(x):
    hi = x.astype(BF16)
    return hi, (x - hi.astype(F32)).astype(BF16)


def dot(a, b, dims=NN):
    return lax.dot_general(a, b, dims, preferred_element_type=F32)


def dot_exact(a, b, dims=NN):
    return lax.dot_general(a, b, dims, precision=lax.Precision.HIGHEST, preferred_element_type=F32)


def legendre_rows(times, legs):
    x = (2.0 * times + 1.0) * (1.0 / TIMES) - 1.0
    before, now = jnp.ones_like(x), x
    yield before
    yield now * math.sqrt(3.0)
    for d in range(1, legs - 1):
        before, now = now, ((2 * d + 1) / (d + 1)) * (x * now) - (d / (d + 1)) * before
        yield now * math.sqrt(2.0 * (d + 1) + 1.0)


def measure_kernel(
    n_grp, legs, updates,
    perturb_in, touched_in, spins_in, accept_in, site_in, time_in, left_in, right_in, weight, routing,
    out, polys, spread, perturb, chosen, spins, accept, site, time, left_proj, right_proj, arrived,
):
    loads = []
    for k, (source, target) in enumerate((
        (time_in, time), (site_in, site), (left_in, left_proj), (right_in, right_proj),
        (touched_in, chosen), (spins_in, spins), (accept_in, accept), (perturb_in, perturb),
    )):
        loads.append(pltpu.make_async_copy(source, target, arrived.at[k]))
        loads[-1].start()
    order = perturb.shape[1]
    sites, width = left_proj.shape
    q = width // legs
    per = q // n_grp
    rank = chosen.shape[2]
    touched = updates * rank
    for load in loads[:4]:
        load.wait()
    for d, row in enumerate(legendre_rows(time[...].astype(F32), legs)):
        polys[d : d + 1, :] = row
    onehot = (lax.broadcasted_iota(jnp.int32, (sites, order), 0) == site[...]).astype(BF16)
    onehot2 = jnp.concatenate([onehot, onehot], axis=0)
    vectors = []
    for table in (left_proj, right_proj):
        hi, lo = split(table[...])
        spread[...] = dot(jnp.concatenate([hi, lo], axis=0), onehot2, TN)
        total = jnp.zeros((q, order), F32)
        for d in range(legs):
            total = total + spread[d * q : (d + 1) * q, :] * polys[d : d + 1, :]
        vectors.append(total)
    left_vec, right_vec = vectors

    for load in loads[4:]:
        load.wait()
    square = lax.broadcasted_iota(jnp.int32, (rank, rank), 0) == lax.broadcasted_iota(
        jnp.int32, (rank, rank), 1
    )

    def column(rows):
        parts = [
            jnp.sum(jnp.where(square, rows[u : u + 1, :].astype(F32), 0.0), axis=1, keepdims=True)
            for u in range(updates)
        ]
        return jnp.concatenate(parts, axis=0)

    index = column(chosen[0]).astype(jnp.int32)
    gammas = column(accept[0].astype(F32) * jnp.where(spins[0] == 1, 0.6, -0.4))
    select = (lax.broadcasted_iota(jnp.int32, (touched, order), 1) == index).astype(BF16)
    p_hi, p_lo = split(perturb[0])
    l_hi, l_lo = split(left_vec)
    r_hi, r_lo = split(right_vec)
    rows = jnp.concatenate([select, r_hi, r_lo], axis=0)
    cols = jnp.concatenate([select, l_hi, l_lo], axis=0)
    by_rows = dot(rows, p_hi) + dot(rows, p_lo)
    by_cols = dot(cols, p_hi, NT) + dot(cols, p_lo, NT)
    p_rows, p_cols = by_rows[:touched], by_cols[:touched]
    g = by_rows[touched : touched + q] + by_rows[touched + q :]
    w = left_vec + by_cols[touched : touched + q] + by_cols[touched + q :]

    def picked(x):
        hi, lo = split(x)
        return dot(hi, select, NT) + dot(lo, select, NT)

    kernel = picked(p_rows)
    overlap = kernel + dot(select, select, NT)
    eye = (
        lax.broadcasted_iota(jnp.int32, (touched, touched), 0)
        == lax.broadcasted_iota(jnp.int32, (touched, touched), 1)
    ).astype(F32)
    s = jnp.zeros((touched, touched), F32)
    for u in range(updates):
        part = slice(u * rank, (u + 1) * rank)
        if u == 0:
            first, second = eye[:, part], eye[part, :]
        else:
            first = eye[:, part] - dot_exact(s, overlap[:, part])
            second = eye[part, :] - dot_exact(kernel[part, :], s)
        s = s + dot_exact(first, gammas[part, :] * second)
    z = dot_exact(picked(w), s, NT)
    v = dot_exact(picked(g), s)
    left_image = w - dot_exact(z, p_cols)
    v_hi, v_lo = split(v)
    right_image = right_vec + g - (dot_exact(v, p_rows) + dot(v_hi, select) + dot(v_lo, select))

    tiles = order // LANES
    site_f, time_f = site[...].astype(F32), time[...].astype(F32)
    for t in range(tiles):
        lanes = slice(t * LANES, (t + 1) * LANES)
        for k in range(n_grp):
            mine = slice(k * per, (k + 1) * per)
            out[k, t * 2 * per : t * 2 * per + per, :] = left_image[mine, lanes]
            out[k, t * 2 * per + per : (t + 1) * 2 * per, :] = right_image[mine, lanes]
            base = tiles * 2 * per
            out[k, base + t : base + t + 1, :] = site_f[:, lanes]
            out[k, base + tiles + t : base + tiles + t + 1, :] = time_f[:, lanes]
    base = tiles * (2 * per + 2)
    for k in range(n_grp):
        out[k, base : base + 4, :] = jnp.full((4, LANES), weight[0], F32)
        out[k, base + 4 : base + 8, :] = jnp.full((4, LANES), routing[0, 0].astype(F32), F32)


def accumulate_kernel(
    legs, per, tiles, blocks,
    gathered, total_hbm, out, polys, left_rows, right_rows, table, images, right_pair, held, arrived,
):
    n_mem, n_grp = gathered.shape[0], gathered.shape[1]
    walkers = n_mem * n_grp
    pairs = total_hbm.shape[2] // LANES
    step = pl.program_id(0)
    mem = lax.axis_index("mem")
    meta = tiles * 2 * per
    last = meta + 2 * tiles

    def load(at):
        k, b = at // blocks, at % blocks
        rows = pl.ds(pl.multiple_of(b * LANES, LANES), LANES)
        return pltpu.make_async_copy(total_hbm.at[k, rows, :], held.at[at], arrived.at[at])

    @pl.when(step == 0)
    def _():
        lax.fori_loop(0, per * blocks, lambda at, carry: (load(at).start(), carry)[1], 0)

        def member(m, carry):
            times = jnp.concatenate(
                [gathered[m, g, meta + tiles : last, :] for g in range(n_grp)], axis=0
            )
            for d, row in enumerate(legendre_rows(times, legs)):
                polys[d * n_grp * tiles : (d + 1) * n_grp * tiles, :] = row
            for g in range(n_grp):
                walker = m * n_grp + g
                own = gathered[m, g, last + 4 : last + 5, :]
                weight = gathered[m, g, last : last + 1, :]
                same = jnp.zeros_like(own)
                for other in range(n_mem):
                    same = same + jnp.where(
                        gathered[other, g, last + 4 : last + 5, :] == own,
                        gathered[other, g, last : last + 1, :],
                        0.0,
                    )
                factor = weight / same
                for t in range(tiles):
                    lanes = slice(t * LANES, (t + 1) * LANES)
                    site = gathered[m, g, meta + t : meta + t + 1, :].astype(jnp.int32)
                    odd, pair = site % 2, site // 2
                    p = polys[pl.ds(g * tiles + t, legs, stride=n_grp * tiles), :]
                    p = jnp.concatenate(
                        [jnp.where(odd == 0, p, 0.0), jnp.where(odd == 1, p, 0.0)], axis=0
                    )
                    p_hi, p_lo = split(p)
                    table[g % 2, :LANES, lanes] = p_hi
                    table[g % 2, LANES:, lanes] = p_lo
                    image = gathered[m, g, t * 2 * per : (t + 1) * 2 * per, :]
                    hi = image.astype(BF16).astype(F32)
                    lo = image - hi
                    at = pair == lax.broadcasted_iota(jnp.int32, (pairs, LANES), 0)
                    at_own = pair == mem * blocks + lax.broadcasted_iota(jnp.int32, (8, LANES), 0)
                    half = per * pairs + per * 8
                    for part, value in ((0, hi), (1, lo)):
                        rows = [jnp.where(at, value[per + k : per + k + 1, :], 0.0) for k in range(per)]
                        rows += [jnp.where(at_own, value[k : k + 1, :], 0.0) for k in range(per)]
                        images[g % 2, part * half : (part + 1) * half, lanes] = jnp.concatenate(
                            rows, axis=0
                        ).astype(BF16)
                half = per * pairs + per * 8
                both = dot(images[g % 2], table[g % 2], NT)
                summed = both[:half, :LANES] + both[:half, LANES:] + both[half:, :LANES]
                for k in range(per):
                    right_rows[pl.ds(k * pairs * walkers + walker, pairs, stride=walkers), :] = (
                        summed[k * pairs : (k + 1) * pairs, :]
                    )
                    for b in range(blocks):
                        at_row = per * pairs + k * 8 + b
                        left_rows[pl.ds((k * blocks + b) * walkers + walker, 1), :] = (
                            summed[at_row : at_row + 1, :] * factor
                        )
            return carry

        lax.fori_loop(0, n_mem, member, 0)

    transfer, block = step // blocks, step % blocks

    @pl.when(block == 0)
    def _():
        for c in range(pairs):
            start = pl.multiple_of((transfer * pairs + c) * walkers, walkers)
            hi, lo = split(right_rows[pl.ds(start, walkers), :])
            lanes = slice(c * LANES, (c + 1) * LANES)
            right_pair[:walkers, lanes] = hi
            right_pair[walkers : 2 * walkers, lanes] = lo
            right_pair[2 * walkers :, lanes] = hi

    start = pl.multiple_of((transfer * blocks + block) * walkers, walkers)
    hi, lo = split(left_rows[pl.ds(start, walkers), :])
    left = jnp.concatenate([hi, hi, lo], axis=0)
    load(step).wait()
    out[0] = held[step] + dot(left, right_pair[...], TN)


def gather_kernel(n_grp, n_mem, payload, out, grp_send, grp_recv, ring_send, ring_recv, own_sem):
    grp, mem = lax.axis_index("grp"), lax.axis_index("mem")
    half = n_mem // 2

    def at_place(place):
        return jnp.where(place < half, 2 * place, 2 * (n_mem - 1 - place) + 1)

    place = jnp.where(mem % 2 == 0, mem // 2, n_mem - 1 - mem // 2)
    peers = [
        ((grp // 2 + j // 2) % (n_grp // 2)) * 2 + (grp % 2 + j % 2) % 2 for j in range(n_grp)
    ]
    sides = [at_place((place + 1) % n_mem), at_place((place + n_mem - 1) % n_mem)]

    barrier = pltpu.get_barrier_semaphore()
    for peer in peers[1:]:
        pl.semaphore_signal(barrier, inc=1, device_id=(peer, mem), device_id_type=MESH)
    for side in sides:
        pl.semaphore_signal(barrier, inc=1, device_id=(grp, side), device_id_type=MESH)
    pl.semaphore_wait(barrier, n_grp + 1)

    def runs(step, j):
        if step < half - 1:
            return (0, 1)
        if step == half - 1:
            return (j % 2,)
        return ()

    started = []

    def pass_on(step, j, side, source):
        origin = at_place((place + (n_mem - step if side == 0 else step)) % n_mem)
        copy = pltpu.make_async_remote_copy(
            src_ref=payload.at[peers[j]] if source is None else source,
            dst_ref=out.at[origin, peers[j]],
            send_sem=ring_send.at[side, step, j],
            recv_sem=ring_recv.at[side, step, j],
            device_id=(grp, sides[side]),
            device_id_type=MESH,
        )
        copy.start()
        started.append(copy)

    crossing = []
    for j in range(1, n_grp):
        copy = pltpu.make_async_remote_copy(
            src_ref=payload.at[peers[j]],
            dst_ref=out.at[mem, grp],
            send_sem=grp_send.at[peers[j]],
            recv_sem=grp_recv.at[grp],
            device_id=(peers[j], mem),
            device_id_type=MESH,
        )
        copy.start()
        crossing.append(copy)
    for side in runs(0, 0):
        pass_on(0, 0, side, None)
    own = pltpu.make_async_copy(payload.at[grp], out.at[mem, grp], own_sem)
    own.start()
    for j in range(1, n_grp):
        block = out.at[mem, peers[j]]
        pltpu.make_async_copy(block, block, grp_recv.at[peers[j]]).wait()
        for side in runs(0, j):
            pass_on(0, j, side, block)
    for step in range(1, half + 1):
        for j in range(n_grp):
            for side in runs(step - 1, j):
                origin = at_place((place + (n_mem - step if side == 0 else step)) % n_mem)
                block = out.at[origin, peers[j]]
                pltpu.make_async_copy(block, block, ring_recv.at[side, step - 1, j]).wait()
                if side in runs(step, j):
                    pass_on(step, j, side, block)
    own.wait()
    for copy in crossing + started:
        copy.wait_send()


def gather_payload(payload, n_grp, n_mem):
    half = n_mem // 2
    vmem = pl.BlockSpec(memory_space=pltpu.VMEM)
    return pl.pallas_call(
        functools.partial(gather_kernel, n_grp, n_mem),
        out_shape=jax.ShapeDtypeStruct((n_mem, *payload.shape), F32),
        in_specs=[pl.BlockSpec(memory_space=pl.ANY)],
        out_specs=vmem,
        scratch_shapes=[
            pltpu.SemaphoreType.DMA((n_grp,)),
            pltpu.SemaphoreType.DMA((n_grp,)),
            pltpu.SemaphoreType.DMA((2, half, n_grp)),
            pltpu.SemaphoreType.DMA((2, half, n_grp)),
            pltpu.SemaphoreType.DMA,
        ],
        compiler_params=pltpu.CompilerParams(
            collective_id=0, has_side_effects=True, vmem_limit_bytes=(20 if n_mem > 8 else 8) * 2**20
        ),
    )(payload)


def per_device(
    n_grp, n_mem,
    perturb, touched_vertex_index, proposed_spin_values, accept,
    vertex_site_index, vertex_time_index, left_proj, right_proj,
    weights, routing, vertex_function_total,
):
    order = perturb.shape[1]
    sites, width = left_proj.shape
    per, rows, cols = vertex_function_total.shape
    legs = cols // sites
    updates, rank = touched_vertex_index.shape[1:]
    tiles = order // LANES
    blocks = rows // LANES
    payload_rows = tiles * (2 * per + 2) + 8
    vmem = pl.BlockSpec(memory_space=pltpu.VMEM)
    smem = pl.BlockSpec(memory_space=pltpu.SMEM)
    hbm = pl.BlockSpec(memory_space=pl.ANY)
    loaded = (
        perturb, touched_vertex_index, proposed_spin_values, accept,
        vertex_site_index, vertex_time_index, left_proj, right_proj,
    )
    payload = pl.pallas_call(
        functools.partial(measure_kernel, n_grp, legs, updates),
        out_shape=jax.ShapeDtypeStruct((n_grp, payload_rows, LANES), F32),
        in_specs=[hbm] * 8 + [smem] * 2,
        out_specs=vmem,
        scratch_shapes=[pltpu.VMEM((legs, order), F32), pltpu.VMEM((width, order), F32)]
        + [pltpu.VMEM(x.shape, x.dtype) for x in loaded]
        + [pltpu.SemaphoreType.DMA((len(loaded),))],
        compiler_params=pltpu.CompilerParams(vmem_limit_bytes=67043328),
    )(*loaded, weights, routing)
    gathered = gather_payload(payload, n_grp, n_mem)
    walkers = n_grp * n_mem
    pairs = cols // LANES
    return pl.pallas_call(
        functools.partial(accumulate_kernel, legs, per, tiles, blocks),
        grid=(per * blocks,),
        out_shape=jax.ShapeDtypeStruct(vertex_function_total.shape, F32),
        in_specs=[vmem, hbm],
        out_specs=pl.BlockSpec((1, LANES, cols), lambda i: (i // blocks, i % blocks, 0)),
        scratch_shapes=[
            pltpu.VMEM((legs * n_grp * tiles, LANES), F32),
            pltpu.VMEM((per * blocks * walkers, LANES), F32),
            pltpu.VMEM((per * pairs * walkers, LANES), F32),
            pltpu.VMEM((2, 2 * LANES, order), BF16),
            pltpu.VMEM((2, 2 * (per * pairs + per * 8), order), BF16),
            pltpu.VMEM((3 * walkers, cols), BF16),
            pltpu.VMEM((per * blocks, LANES, cols), F32),
            pltpu.SemaphoreType.DMA((per * blocks,)),
        ],
        compiler_params=pltpu.CompilerParams(vmem_limit_bytes=50 * 2**20),
    )(gathered, vertex_function_total)


def solution(mesh):
    in_specs = (
        P(("grp", "mem"), None, None),
        P(("grp", "mem"), None, None),
        P(("grp", "mem"), None, None),
        P(("grp", "mem"), None, None),
        P(("grp", "mem"), None),
        P(("grp", "mem"), None),
        P(),
        P(),
        P(("grp", "mem")),
        P(("grp", "mem"), None),
        P("grp", "mem", None),
    )
    return jax.shard_map(
        functools.partial(per_device, mesh.shape["grp"], mesh.shape["mem"]),
        mesh=mesh, in_specs=in_specs, out_specs=P("grp", "mem", None), check_vma=False,
    )
```
